32 devices in a mesh: dp: 16 (over z, y, x), feat: 2 (over core).
Axes of the slice: x: 2, y: 2, z: 4, core: 2. Of those that a mesh axis runs over, the one named last changes fastest.
Arguments:
- embeddings: bfloat16 [81920, 2048], P('dp', 'feat'), may hold values from -80 to 80
- slot_image: int32 [81920], P('dp'), may hold values from 0 to 8191, as said below
- slot_view: int32 [81920], P('dp'), may hold values from 0 to 10, as said below
- pair_table: int32 [2, 2], replicated, may hold values from 0 to 9, as said below
Outputs:
- correlation: float32 [2, 2048, 2048], P(None, 'feat', 'dp')
The draws below stay inside these ranges and needn't reach their ends.
Inputs may be any that keep to these rules, and one draw needn't show every extreme that they name: `slot_image`: image ids of dp index d run from d * 512 to (d + 1) * 512 - 1. Each image has views 0 and 1 and local views 2 to 1 + k with k from 1 to 8; the first image of every dp index has all 10 views; every (image, view) stands in one slot at most; empty slots name an image of their own dp index. `slot_view`: empty slots carry view 10 and come after the used slots of their dp index; the last dp index fills all its slots. `pair_table`: each pair's first view is global (0 or 1) and its second view differs from it.
All inputs are finite; a program needn't handle non-finite values.
Results may differ from the reference program's by a relative error of at most 0.00035.
Values may be sent and summed in bfloat16 or wider, within the bound.
No kernel may reach another device: no remote copies, remote signals or barrier semaphores. Data moves between devices by JAX's collectives and lax.ppermute only.
A program may use at most 64 MiB of HBM per device.

```python
import jax
import jax.numpy as jnp
from jax import lax

WIN = 2048
IMG_DEV = 512
LOCALS = 8
PAIRS = 2
VIEWS = 10
ROWS_DEV = 5120
IMAGES = 8192
TOTAL_ROWS = 81920


def crop_lists(key):
    device_count = IMAGES // IMG_DEV
    first_key, second_key = jax.random.split(key)
    device_index = jnp.arange(device_count, dtype=jnp.int32)[:, None]
    upper_bound = 1 + 7 * device_index // max(device_count - 1, 1)
    raw_bits = jax.random.randint(first_key, (device_count, IMG_DEV), 0, 1 << 20)
    local_counts = raw_bits % upper_bound + 1
    local_counts = jnp.where(device_index == device_count - 1, LOCALS, local_counts)
    local_counts = local_counts.at[:, 0].set(LOCALS)
    view_grid = jnp.arange(VIEWS, dtype=jnp.int32)[None, None, :]
    usable = (view_grid < 2 + local_counts[:, :, None]).reshape(device_count, ROWS_DEV)
    device_keys = jax.random.split(second_key, device_count)
    shuffled = jax.vmap(lambda one_key: jax.random.permutation(one_key, ROWS_DEV))(device_keys).astype(jnp.int32)
    sort_score = jnp.where(usable, shuffled, ROWS_DEV + jnp.arange(ROWS_DEV, dtype=jnp.int32)[None, :])
    sorted_slots = jnp.argsort(sort_score, axis=1, stable=True).astype(jnp.int32)
    usable_sorted = jnp.take_along_axis(usable, sorted_slots, axis=1)
    image_ids = device_index * IMG_DEV + sorted_slots // VIEWS
    view_ids = jnp.where(usable_sorted, sorted_slots % VIEWS, VIEWS)
    return (image_ids.reshape(-1).astype(jnp.int32), view_ids.reshape(-1).astype(jnp.int32))


def draw_slot_image(key, part):
    return crop_lists(jax.random.fold_in(key, 11))[0]


def draw_slot_view(key, part):
    return crop_lists(jax.random.fold_in(key, 11))[1]


def draw_pair_table(key, part):
    first_key, second_key, third_key = jax.random.split(jax.random.fold_in(key, 13), 3)
    global_view = jax.random.randint(first_key, (PAIRS,), 0, 2)
    other_view = (global_view + 1 + jax.random.randint(second_key, (PAIRS,), 0, VIEWS - 1)) % VIEWS
    chosen = jax.random.randint(third_key, (), 0, PAIRS)
    is_chosen = jnp.arange(PAIRS, dtype=jnp.int32) == chosen
    global_view = jnp.where(is_chosen, 0, global_view)
    other_view = jnp.where(is_chosen, VIEWS - 1, other_view)
    return jnp.stack([global_view, other_view], axis=1).astype(jnp.int32)


def draw_embeddings(key, part):
    image_ids, view_ids = crop_lists(jax.random.fold_in(key, 11))
    base_key = jax.random.fold_in(key, 12)
    latent_key, noise_key, column_key = jax.random.split(base_key, 3)
    latent = jax.random.truncated_normal(latent_key, -4.0, 4.0, (IMAGES, WIN), jnp.float32)
    column_scale = jnp.exp(jax.random.uniform(column_key, (WIN,), jnp.float32, jnp.log(0.5), jnp.log(5.0)))
    noise = jax.random.truncated_normal(noise_key, -4.0, 4.0, (TOTAL_ROWS, WIN), jnp.float32)
    values = (jnp.take(latent, image_ids, axis=0) + 0.6 * noise) * column_scale
    return values.astype(jnp.bfloat16)


def setup_inputs(seed: int = 0) -> dict:
    key_of = jax.random.split(jax.random.key(seed), 5)
    embeddings = draw_embeddings(jax.random.fold_in(key_of[4], 71), 0)
    slot_image = draw_slot_image(jax.random.fold_in(key_of[4], 71), 0)
    slot_view = draw_slot_view(jax.random.fold_in(key_of[4], 71), 0)
    pair_table = draw_pair_table(jax.random.fold_in(key_of[4], 71), 0)
    return {"embeddings": embeddings, "slot_image": slot_image, "slot_view": slot_view, "pair_table": pair_table}


EPS = 1e-05

def locate(slot_image, slot_view, view_id):
    positions = jnp.arange(slot_view.shape[0], dtype=jnp.int32) + 1
    marked = jnp.where(slot_view == view_id, positions, jnp.zeros((), jnp.int32))
    return jnp.zeros((IMAGES,), jnp.int32).at[slot_image].max(marked) - 1

def pick_rows(embeddings, slots, present):
    taken = jnp.take(embeddings, jnp.maximum(slots, 0).astype(jnp.int32), axis=0)
    return jnp.where(present[:, None], taken, jnp.zeros((), embeddings.dtype))

def reference(embeddings, slot_image, slot_view, pair_table):
    outputs = []
    for pair_index in range(PAIRS):
        first = locate(slot_image, slot_view, pair_table[pair_index, 0])
        second = locate(slot_image, slot_view, pair_table[pair_index, 1])
        present = (first >= 0) & (second >= 0)
        first_rows = pick_rows(embeddings, first, present)
        second_rows = pick_rows(embeddings, second, present)
        total = jnp.sum(present.astype(jnp.float32))
        first_wide = first_rows.astype(jnp.float32)
        second_wide = second_rows.astype(jnp.float32)
        mean_first = lax.optimization_barrier(jnp.sum(first_wide, axis=0)) / total
        mean_second = lax.optimization_barrier(jnp.sum(second_wide, axis=0)) / total
        square_first = lax.optimization_barrier(jnp.sum(first_wide * first_wide, axis=0)) / total
        square_second = lax.optimization_barrier(jnp.sum(second_wide * second_wide, axis=0)) / total
        spread_first = jnp.sqrt(square_first - mean_first * mean_first + EPS)
        spread_second = jnp.sqrt(square_second - mean_second * mean_second + EPS)
        cross = jnp.dot(first_rows.T, second_rows, preferred_element_type=jnp.float32)
        block = (cross / total - mean_first[:, None] * mean_second[None, :]) / (spread_first[:, None] * spread_second[None, :])
        outputs.append(block)
    return jnp.stack(outputs, axis=0)
```

```python
import jax
import jax.numpy as jnp
from jax import lax
from jax.sharding import PartitionSpec as P

VIEWS = 10
PAIRS = 2
EPS = 1e-05
CHUNKS = 2


def select_rows(embeddings, local_image, slot_view, view_id, images):
    image_grid = jnp.arange(images, dtype=jnp.int32)[:, None]
    selection = ((local_image[None, :] == image_grid) & (slot_view[None, :] == view_id)).astype(
        jnp.bfloat16
    )
    found = jnp.sum(selection.astype(jnp.float32), axis=1) > 0.5
    rows = jnp.dot(selection, embeddings, preferred_element_type=jnp.float32).astype(jnp.bfloat16)
    return rows, found


def swap(value, axis, mask):
    size = lax.axis_size(axis)
    return lax.ppermute(value, axis, [(k, k ^ mask) for k in range(size)])


def bits_of(size):
    return size.bit_length() - 1


def scale_of(sums, spread, count):
    floor = 1e-4 * (spread + sums * sums / count)
    return 128.0 * lax.rsqrt(jnp.maximum(spread, floor) + 1e-30)


def pack(parts):
    flat = jnp.concatenate([part.reshape(-1) for part in parts])
    return jnp.pad(flat, (0, -flat.shape[0] % 1024)).reshape(-1, 128)


def unpack(packed, likes):
    flat = packed.reshape(-1)
    out, offset = [], 0
    for like in likes:
        size = like.size
        out.append(flat[offset : offset + size].reshape(like.shape))
        offset += size
    return out


def take_blocks(rows, block, starts):
    return jnp.concatenate(
        [lax.dynamic_slice_in_dim(rows, start * block, block, 1) for start in starts], axis=1
    )


def moments(rows, count):
    wide = rows.astype(jnp.float32)
    sums = jnp.sum(wide, axis=0)
    squares = jnp.sum(wide * wide, axis=0)
    return sums, squares - sums * sums / count


def pair_blocks(first_rows, second_rows, images_here, order):
    dp, feat = lax.axis_size("dp"), lax.axis_size("feat")
    me, core = lax.axis_index("dp"), lax.axis_index("feat")
    width = first_rows.shape[1]
    block = width * feat // dp
    low = bits_of(width // block)
    high = bits_of(feat)
    near, next_bit = order[0], order[1]
    mine = [(me >> bit) & 1 for bit in range(low + high)]

    def columns(near_value, next_value):
        rest = [bit for bit in range(low) if bit not in (near, next_bit)]
        starts = []
        for code in range(1 << len(rest)):
            start = (near_value << near) + (next_value << next_bit)
            for place, bit in enumerate(rest):
                start = start + (((code >> place) & 1) << bit)
            starts.append(start)
        return take_blocks(second_rows, block, starts)

    rest_bits = [bit for bit in range(low) if bit not in (near, next_bit)][::-1]
    other_near, other_next = 1 - mine[near], 1 - mine[next_bit]
    away = jnp.concatenate([columns(other_near, other_next), columns(other_near, mine[next_bit])], 1)
    kept = jnp.concatenate([columns(mine[near], other_next), columns(mine[near], mine[next_bit])], 1)
    come = swap(away, "dp", 1 << near)
    count = images_here + swap(jnp.full((8, 128), images_here), "dp", 1 << near)[0, 0]
    chunk = width // CHUNKS
    firsts = []
    for c in range(CHUNKS):
        piece = first_rows[:, c * chunk : (c + 1) * chunk]
        firsts.append(jnp.concatenate([piece, swap(piece, "dp", 1 << near)], axis=0))
    kept_all = jnp.stack([kept] + [swap(kept, "feat", s) for s in range(1, feat)], 0)
    come_all = jnp.stack([come] + [swap(come, "feat", s) for s in range(1, feat)], 0)
    seconds = jnp.concatenate([kept_all, come_all], axis=1)
    half = seconds.shape[2] // 2
    shape = (2,) * high + (2,) * len(rest_bits) + (block,)

    def second_moments(rows):
        wide = rows.astype(jnp.float32)
        sums = jnp.sum(wide, axis=1)
        squares = jnp.sum(wide * wide, axis=1)
        return sums.reshape(shape), (squares - sums * sums / count).reshape(shape)

    go_rows, stay_rows = seconds[:, :, :half], seconds[:, :, half:]
    go_stats, stay_stats = second_moments(go_rows), second_moments(stay_rows)
    first_stats = [moments(piece, count) for piece in firsts]

    def product(rows, piece, second_sums, first_sums):
        value = lax.dot_general(
            rows.reshape(feat, rows.shape[1], half),
            piece,
            (((1,), (0,)), ((), ())),
            preferred_element_type=jnp.float32,
        ).reshape(shape + (chunk,))
        return value - second_sums[..., None] * (first_sums / count)

    def narrow(value, second_scale, first_scale):
        scaled = value * second_scale[..., None] * first_scale
        return jnp.clip(scaled, -60000.0, 60000.0).astype(jnp.float16)

    go = [
        product(go_rows, piece, go_stats[0], stats[0]) for piece, stats in zip(firsts, first_stats)
    ]
    stay = [
        product(stay_rows, piece, stay_stats[0], stats[0])
        for piece, stats in zip(firsts, first_stats)
    ]
    axes = list(range(low, low + high))[::-1] + rest_bits
    for step, bit in enumerate(order[1:]):
        if step:
            axis = axes.index(bit)
            axes.remove(bit)
            keep_at = mine[bit] ^ ((core >> (bit - low)) & 1) if bit >= low else mine[bit]

            def part(value, at):
                return lax.dynamic_index_in_dim(value, at, axis, keepdims=False)

            go = [part(value, 1 - keep_at) for value in stay]
            go_stats = [part(value, 1 - keep_at) for value in stay_stats]
            stay = [part(value, keep_at) for value in stay]
            stay_stats = [part(value, keep_at) for value in stay_stats]
        go_scale = scale_of(*go_stats, count)
        sent = [
            swap(narrow(value, go_scale, scale_of(*stats, count)), "dp", 1 << bit)
            for value, stats in zip(go, first_stats)
        ]
        message = pack([*go_stats, *[v for stats in first_stats for v in stats], count[None]])
        answer = unpack(
            swap(message, "dp", 1 << bit),
            [*go_stats, *[v for stats in first_stats for v in stats], count[None]],
        )
        there_second, there_first, there_count = answer[:2], answer[2:-1], answer[-1][0]
        both = count + there_count
        weight = count * there_count / both
        second_scale = 1.0 / scale_of(*there_second, there_count)
        second_step = stay_stats[0] / count - there_second[0] / there_count
        merged, merged_first = [], []
        for c in range(CHUNKS):
            sums, spread = first_stats[c]
            far_sums, far_spread = there_first[2 * c], there_first[2 * c + 1]
            first_scale = 1.0 / scale_of(far_sums, far_spread, there_count)
            first_step = sums / count - far_sums / there_count
            merged.append(
                stay[c]
                + sent[c].astype(jnp.float32) * second_scale[..., None] * first_scale
                + (weight * second_step)[..., None] * first_step
            )
            merged_first.append(
                (sums + far_sums, spread + far_spread + weight * first_step * first_step)
            )
        stay_stats = [
            stay_stats[0] + there_second[0],
            stay_stats[1] + there_second[1] + weight * second_step * second_step,
        ]
        stay, first_stats, count = merged, merged_first, both
    second_root = jnp.sqrt(stay_stats[1] / count + EPS)
    blocks = []
    for value, stats in zip(stay, first_stats):
        first_root = jnp.sqrt(stats[1] / count + EPS)
        blocks.append((value / count / (second_root[:, None] * first_root[None, :])).T)
    return jnp.concatenate(blocks, axis=0)


def local(embeddings, slot_image, slot_view, pair_table):
    images = embeddings.shape[0] // VIEWS
    local_image = slot_image - lax.axis_index("dp") * images
    outputs = []
    for pair_index in range(PAIRS):
        first_taken, first_found = select_rows(
            embeddings, local_image, slot_view, pair_table[pair_index, 0], images
        )
        second_taken, second_found = select_rows(
            embeddings, local_image, slot_view, pair_table[pair_index, 1], images
        )
        present = first_found & second_found
        zero = jnp.zeros((), jnp.bfloat16)
        first_rows = jnp.where(present[:, None], first_taken, zero)
        second_rows = jnp.where(present[:, None], second_taken, zero)
        order = list(range(bits_of(lax.axis_size("dp"))))
        if pair_index % 2:
            order[:2] = order[1::-1]
        outputs.append(
            pair_blocks(first_rows, second_rows, jnp.sum(present.astype(jnp.float32)), order)
        )
    return jnp.stack(outputs, axis=0)


def solution(mesh):
    in_specs = (P("dp", "feat"), P("dp"), P("dp"), P())
    out_specs = P(None, "feat", "dp")
    return jax.shard_map(local, mesh=mesh, in_specs=in_specs, out_specs=out_specs, check_vma=False)
```

```python
import jax
import jax.numpy as jnp
from jax import lax
from jax.experimental import pallas as pl
from jax.experimental.pallas import tpu as pltpu
from jax.sharding import PartitionSpec as P

VIEWS = 10
PAIRS = 2
EPS = 1e-05
CHUNKS = 2
STEPS = 10
UNIT = 16384.0


def select_kernel(image_ref, view_ref, pair_ref, emb_ref, f0, s0, f1, s1, stats0, stats1,
                  raw, wide, held, turned, slots, sem, slot_sem):
    outs = (f0, s0, f1, s1)
    stats = (stats0, stats1)
    rows, width = raw.shape
    pieces = width // 128
    images = f0.shape[0]
    step = rows // STEPS

    def fetch(k):
        part = pl.ds(k * step, step)
        return pltpu.make_async_copy(emb_ref.at[part, :], raw.at[part, :], sem.at[k])

    for k in range(STEPS):
        fetch(k).start()
    image = image_ref[...] - lax.axis_index("dp") * images
    view = view_ref[...]
    groups = images // 16
    upper = lax.broadcasted_iota(jnp.int32, (groups, rows), 0)
    hits = jnp.where(upper == jnp.right_shift(image, 4), 1.0, 0.0).astype(jnp.bfloat16)
    lower = jnp.bitwise_and(image, 15) * 16 + view
    line = lax.broadcasted_iota(jnp.int32, (96, 1), 0)
    place = lax.broadcasted_iota(jnp.int32, (32, rows), 1)
    values = jnp.concatenate(
        [jnp.right_shift(place, 6), jnp.bitwise_and(place, 63), jnp.ones_like(place)], 0
    ).astype(jnp.float32)
    found = []
    for role in range(2):
        wanted = jnp.bitwise_and(line, 15) * 16 + jnp.where(
            jnp.bitwise_and(line, 16) == 0, pair_ref[0, role], pair_ref[1, role]
        )
        marks = jnp.where(wanted == lower, values, 0.0).astype(jnp.bfloat16)
        marks = jnp.concatenate([marks, jnp.zeros((32, rows), jnp.bfloat16)], 0)
        found.append(
            lax.dot_general(
                hits, marks, (((1,), (1,)), ((), ())), preferred_element_type=jnp.float32
            )
        )
    both = pltpu.roll(found[0], 64, 1) * pltpu.roll(found[1], 64, 1) > 0.5
    for ref in stats:
        ref[...] = jnp.zeros_like(ref)
    lanes = lax.broadcasted_iota(jnp.int32, (groups, 128), 1)
    for p in range(2):
        mine = both & (lanes >= 16 * p) & (lanes < 16 * p + 16)
        amount = jnp.sum(jnp.sum(mine.astype(jnp.float32), axis=0, keepdims=True), axis=1, keepdims=True)
        stats[p][0:1, width : width + 128] = jnp.broadcast_to(amount, (1, 128))
    for role in range(2):
        slot = jnp.minimum(found[role] * 64.0 + pltpu.roll(found[role], 96, 1), float(rows))
        turned[role * groups : (role + 1) * groups, :] = jnp.where(both, slot, float(rows)).astype(
            jnp.int32
        )
    to_scalar = pltpu.make_async_copy(turned, slots, slot_sem)
    to_scalar.start()
    wide[pl.ds(rows * pieces, pieces), :] = jnp.zeros((pieces, 128), jnp.float32)
    for k in range(STEPS):
        fetch(k).wait()

        def widen(t, carry):
            start = pl.multiple_of(k * step + t * 32, 32)
            for c in range(pieces):
                wide[pl.ds(start * pieces + c, 32, stride=pieces), :] = raw[
                    pl.ds(start, 32), c * 128 : (c + 1) * 128
                ].astype(jnp.float32)
            return carry

        lax.fori_loop(0, step // 32, widen, 0)
    to_scalar.wait()

    def gather(t, carry):
        for u in range(16):
            n = t * 16 + u
            for k in range(4):
                slot = slots[(k % 2) * groups + t, (k // 2) * 16 + u]
                held[pl.ds(pl.multiple_of((k * images + n) * pieces, pieces), pieces), :] = wide[
                    pl.ds(pl.multiple_of(slot * pieces, pieces), pieces), :
                ]
        return carry

    lax.fori_loop(0, groups, gather, 0)
    for k in range(4):
        for c in range(pieces):

            def emit(t, carry):
                sums, squares = carry
                start = pl.multiple_of(t * 128, 128)
                value = held[pl.ds((k * images + start) * pieces + c, 128, stride=pieces), :]
                outs[k][pl.ds(start, 128), c * 128 : (c + 1) * 128] = value.astype(jnp.bfloat16)
                value = value.reshape(16, 8, 128)
                return sums + value.sum(0), squares + (value * value).sum(0)

            zero = jnp.zeros((8, 128), jnp.float32)
            sums, squares = lax.fori_loop(0, images // 128, emit, (zero, zero))
            at = slice(c * 128, (c + 1) * 128)
            line = 2 * (k % 2)
            stats[k // 2][line : line + 1, at] = jnp.sum(sums, axis=0, keepdims=True)
            stats[k // 2][line + 1 : line + 2, at] = jnp.sum(squares, axis=0, keepdims=True)


def select_all(embeddings, slot_image, slot_view, pair_table, images):
    rows, width = embeddings.shape
    pieces = width // 128
    vmem = pl.BlockSpec(memory_space=pltpu.VMEM)
    return pl.pallas_call(
        select_kernel,
        out_shape=[jax.ShapeDtypeStruct((images, width), jnp.bfloat16)] * 4
        + [jax.ShapeDtypeStruct((8, width + 128), jnp.float32)] * 2,
        in_specs=[vmem, vmem, pl.BlockSpec(memory_space=pltpu.SMEM), pl.BlockSpec(memory_space=pl.ANY)],
        out_specs=[vmem] * 6,
        scratch_shapes=[
            pltpu.VMEM((rows, width), jnp.bfloat16),
            pltpu.VMEM(((rows + 1) * pieces, 128), jnp.float32),
            pltpu.VMEM((4 * pieces * images, 128), jnp.float32),
            pltpu.VMEM((images // 8, 128), jnp.int32),
            pltpu.SMEM((images // 8, 128), jnp.int32),
            pltpu.SemaphoreType.DMA((STEPS,)),
            pltpu.SemaphoreType.DMA,
        ],
        compiler_params=pltpu.CompilerParams(vmem_limit_bytes=60 << 20),
        name="select",
    )(slot_image.reshape(1, -1), slot_view.reshape(1, -1), pair_table, embeddings)


def select_plain(embeddings, slot_image, slot_view, pair_table, images):
    width = embeddings.shape[1]
    local_image = slot_image - lax.axis_index("dp") * images
    image_grid = jnp.arange(images, dtype=jnp.int32)[:, None]
    rows, stats = [], []
    for p in range(PAIRS):
        marks = [
            (local_image[None, :] == image_grid) & (slot_view[None, :] == pair_table[p, role])
            for role in range(2)
        ]
        present = jnp.any(marks[0], axis=1) & jnp.any(marks[1], axis=1)
        lines = []
        for mark in marks:
            taken = jnp.dot(
                (mark & present[:, None]).astype(jnp.bfloat16),
                embeddings,
                preferred_element_type=jnp.float32,
            )
            rows.append(taken.astype(jnp.bfloat16))
            lines += [jnp.sum(taken, axis=0), jnp.sum(taken * taken, axis=0)]
        table = jnp.pad(jnp.stack(lines), ((0, 4), (0, 128)))
        amount = jnp.sum(present.astype(jnp.float32))
        stats.append(table.at[0, width:].set(amount))
    return (*rows, *stats)


def swap(value, axis, mask):
    size = lax.axis_size(axis)
    return lax.ppermute(value, axis, [(k, k ^ mask) for k in range(size)])


def bits_of(size):
    return size.bit_length() - 1


def local(embeddings, slot_image, slot_view, pair_table):
    images = embeddings.shape[0] // VIEWS
    dp, feat = lax.axis_size("dp"), lax.axis_size("feat")
    me, core = lax.axis_index("dp"), lax.axis_index("feat")
    width = embeddings.shape[1]
    tiled = width == 1024 and images % 128 == 0 and embeddings.shape[0] % (32 * STEPS) == 0
    chosen = (select_all if tiled else select_plain)(
        embeddings, slot_image, slot_view, pair_table, images
    )
    block = width * feat // dp
    low, high = bits_of(width // block), bits_of(feat)
    mine = [(me >> bit) & 1 for bit in range(low + high)]
    chunk = width // CHUNKS
    orders = []
    for p in range(PAIRS):
        order = list(range(low + high))
        if p % 2:
            order[:2] = order[1::-1]
        orders.append(order)
    rest_bits = list(range(2, low))[::-1]
    shape = (2,) * high + (2,) * len(rest_bits) + (block,)

    def columns(rows, bits, values):
        parts = []
        for code in range(1 << len(rest_bits)):
            start = sum(value << bit for bit, value in zip(bits, values))
            for place, bit in enumerate(rest_bits[::-1]):
                start = start + (((code >> place) & 1) << bit)
            parts.append(lax.dynamic_slice_in_dim(rows, start * block, block, 1))
        return parts

    def halves(rows, order, near_value):
        far = columns(rows, order[:2], (near_value, 1 - mine[order[1]]))
        return jnp.concatenate(far + columns(rows, order[:2], (near_value, mine[order[1]])), 1)

    def across(value):
        return jnp.stack([value] + [swap(value, "feat", s) for s in range(1, feat)], 0)

    firsts = [chosen[0], chosen[2]]
    seconds = [chosen[1], chosen[3]]
    stats = list(chosen[4:])
    kept = [halves(seconds[p], orders[p], mine[orders[p][0]]) for p in range(PAIRS)]
    away = [halves(seconds[p], orders[p], 1 - mine[orders[p][0]]) for p in range(PAIRS)]
    group = [stats[p] + swap(stats[p], "dp", 1 << orders[p][0]) for p in range(PAIRS)]
    come = [swap(away[p], "dp", 1 << orders[p][0]) for p in range(PAIRS)]
    totals = list(group)
    for step in range(1, low + high):
        totals = [totals[p] + swap(totals[p], "dp", 1 << orders[p][step]) for p in range(PAIRS)]
    pieces = [[firsts[p][:, c * chunk : (c + 1) * chunk] for c in range(CHUNKS)] for p in range(PAIRS)]
    far = [[None] * CHUNKS for _ in range(PAIRS)]
    for c in range(CHUNKS):
        for p in range(PAIRS):
            far[p][c] = swap(pieces[p][c], "dp", 1 << orders[p][0])
    kept_all = [across(kept[p]) for p in range(PAIRS)]
    come_all = [across(come[p]) for p in range(PAIRS)]
    half = kept_all[0].shape[2] // 2

    def multiply(left, right):
        return lax.dot_general(
            left, right, (((1,), (0,)), ((), ())), preferred_element_type=jnp.float32
        )

    vectors = []
    for p in range(PAIRS):
        count, amount = totals[p][0, width], group[p][0, width]
        mean = totals[p][0:4:2, :width] / count
        root = jnp.sqrt(totals[p][1:4:2, :width] / count - mean * mean + EPS)
        first_rate = UNIT / (count * root[0])
        first_shift = group[p][0, :width] - amount * mean[0]
        lines = jnp.stack([group[p][2, :width], mean[1], 1.0 / root[1]])
        lines = halves(lines, orders[p], mine[orders[p][0]])
        lines = across(lines)
        vectors.append((mean[0], first_shift, first_rate, lines))

    def product(p, c, side):
        at = slice(side * half, (side + 1) * half)
        value = multiply(kept_all[p][:, :, at], pieces[p][c]) + multiply(
            come_all[p][:, :, at], far[p][c]
        )
        mean, shift, rate, lines = vectors[p]
        span = slice(c * chunk, (c + 1) * chunk)
        lines = lines[:, :, at, None]
        value = value - lines[:, 0] * mean[span] - lines[:, 1] * shift[span]
        return (value * (lines[:, 2] * rate[span])).reshape(shape + (chunk,))

    def narrow(value):
        return jnp.clip(value, -60000.0, 60000.0).astype(jnp.float16)

    blocks = [[None] * CHUNKS for _ in range(PAIRS)]
    stay = [[None] * CHUNKS for _ in range(PAIRS)]
    for c in range(CHUNKS):
        for p in range(PAIRS):
            sent = swap(narrow(product(p, c, 0)), "dp", 1 << orders[p][1])
            stay[p][c] = product(p, c, 1) + sent.astype(jnp.float32)
    axes = list(range(low, low + high))[::-1] + rest_bits
    for bit in range(2, low + high):
        axis = axes.index(bit)
        axes.remove(bit)
        keep_at = mine[bit] ^ ((core >> (bit - low)) & 1) if bit >= low else mine[bit]
        for c in range(CHUNKS):
            for p in range(PAIRS):
                go = lax.dynamic_index_in_dim(stay[p][c], 1 - keep_at, axis, keepdims=False)
                sent = swap(narrow(go), "dp", 1 << bit)
                own = lax.dynamic_index_in_dim(stay[p][c], keep_at, axis, keepdims=False)
                stay[p][c] = own + sent.astype(jnp.float32)
    return jnp.stack(
        [jnp.concatenate([stay[p][c].T for c in range(CHUNKS)], 0) for p in range(PAIRS)]
    ) * (1.0 / UNIT)


def solution(mesh):
    in_specs = (P("dp", "feat"), P("dp"), P("dp"), P())
    out_specs = P(None, "feat", "dp")
    return jax.shard_map(local, mesh=mesh, in_specs=in_specs, out_specs=out_specs, check_vma=False)
```

```python
import jax
import jax.numpy as jnp
from jax import lax
from jax.experimental import pallas as pl
from jax.experimental.pallas import tpu as pltpu
from jax.sharding import PartitionSpec as P

VIEWS = 10
PAIRS = 2
EPS = 1e-05
CHUNKS = 2
STEPS = 10
UNIT = 16384.0


def swap(value, axis, mask):
    size = lax.axis_size(axis)
    return lax.ppermute(value, axis, [(k, k ^ mask) for k in range(size)])


def bits_of(size):
    return size.bit_length() - 1


def select_kernel(image_ref, view_ref, pair_ref, emb_ref, *refs):
    firsts = (refs[:CHUNKS], refs[CHUNKS : 2 * CHUNKS])
    kept, away, stats = (refs[2 * CHUNKS + k : 2 * CHUNKS + k + 2] for k in (0, 2, 4))
    raw, wide, held, turned, slots, sem, slot_sem = refs[2 * CHUNKS + 6 :]
    rows, width = raw.shape
    pieces = width // 128
    images = firsts[0][0].shape[0]
    step = rows // STEPS

    def fetch(k):
        part = pl.ds(k * step, step)
        return pltpu.make_async_copy(emb_ref.at[part, :], raw.at[part, :], sem.at[k])

    for k in range(STEPS):
        fetch(k).start()
    image = image_ref[...] - lax.axis_index("dp") * images
    view = view_ref[...]
    groups = images // 16
    upper = lax.broadcasted_iota(jnp.int32, (groups, rows), 0)
    hits = jnp.where(upper == jnp.right_shift(image, 4), 1.0, 0.0).astype(jnp.bfloat16)
    lower = jnp.bitwise_and(image, 15) * 16 + view
    line = lax.broadcasted_iota(jnp.int32, (96, 1), 0)
    place = lax.broadcasted_iota(jnp.int32, (32, rows), 1)
    values = jnp.concatenate(
        [jnp.right_shift(place, 6), jnp.bitwise_and(place, 63), jnp.ones_like(place)], 0
    ).astype(jnp.float32)
    found = []
    for role in range(2):
        wanted = jnp.bitwise_and(line, 15) * 16 + jnp.where(
            jnp.bitwise_and(line, 16) == 0, pair_ref[0, role], pair_ref[1, role]
        )
        marks = jnp.where(wanted == lower, values, 0.0).astype(jnp.bfloat16)
        marks = jnp.concatenate([marks, jnp.zeros((32, rows), jnp.bfloat16)], 0)
        found.append(
            lax.dot_general(
                hits, marks, (((1,), (1,)), ((), ())), preferred_element_type=jnp.float32
            )
        )
    both = pltpu.roll(found[0], 64, 1) * pltpu.roll(found[1], 64, 1) > 0.5
    for ref in stats:
        ref[...] = jnp.zeros_like(ref)
    lanes = lax.broadcasted_iota(jnp.int32, (groups, 128), 1)
    for p in range(2):
        mine = both & (lanes >= 16 * p) & (lanes < 16 * p + 16)
        amount = jnp.sum(jnp.sum(mine.astype(jnp.float32), axis=0, keepdims=True), axis=1, keepdims=True)
        stats[p][0:1, width : width + 128] = jnp.broadcast_to(amount, (1, 128))
    for role in range(2):
        slot = jnp.minimum(found[role] * 64.0 + pltpu.roll(found[role], 96, 1), float(rows))
        turned[role * groups : (role + 1) * groups, :] = jnp.where(both, slot, float(rows)).astype(
            jnp.int32
        )
    to_scalar = pltpu.make_async_copy(turned, slots, slot_sem)
    to_scalar.start()
    wide[pl.ds(rows * pieces, pieces), :] = jnp.zeros((pieces, 128), jnp.float32)
    for k in range(STEPS):
        fetch(k).wait()

        def widen(t, carry):
            start = pl.multiple_of(k * step + t * 32, 32)
            for c in range(pieces):
                wide[pl.ds(start * pieces + c, 32, stride=pieces), :] = raw[
                    pl.ds(start, 32), c * 128 : (c + 1) * 128
                ].astype(jnp.float32)
            return carry

        lax.fori_loop(0, step // 32, widen, 0)
    to_scalar.wait()

    def gather(t, carry):
        for u in range(16):
            n = t * 16 + u
            for k in range(4):
                slot = slots[(k % 2) * groups + t, (k // 2) * 16 + u]
                held[pl.ds(pl.multiple_of((k * images + n) * pieces, pieces), pieces), :] = wide[
                    pl.ds(pl.multiple_of(slot * pieces, pieces), pieces), :
                ]
        return carry

    lax.fori_loop(0, groups, gather, 0)
    me = lax.axis_index("dp")
    mine = [jnp.bitwise_and(jnp.right_shift(me, bit), 1) for bit in range(2)]
    span = width // CHUNKS // 128
    for k in range(4):
        p, line = k // 2, 2 * (k % 2)
        for m in range(pieces):
            if k % 2:
                near, over, rest = m // 4, (m // 2) % 2, m % 2
                near_value = mine[p] if near else 1 - mine[p]
                over_value = mine[1 - p] if over else 1 - mine[1 - p]
                c = rest * 4 + near_value * (1 << p) + over_value * (2 >> p)
                out = (kept if near else away)[p]
                lane = (m % 4) * 128
            else:
                c, out, lane = m, firsts[p][m // span], (m % span) * 128

            def emit(t, carry):
                sums, squares = carry
                start = pl.multiple_of(t * 128, 128)
                value = held[pl.ds((k * images + start) * pieces + c, 128, stride=pieces), :]
                out[pl.ds(start, 128), lane : lane + 128] = value.astype(jnp.bfloat16)
                value = value.reshape(16, 8, 128)
                return sums + value.sum(0), squares + (value * value).sum(0)

            zero = jnp.zeros((8, 128), jnp.float32)
            sums, squares = lax.fori_loop(0, images // 128, emit, (zero, zero))
            at = pl.ds(pl.multiple_of(c * 128, 128), 128)
            stats[p][line : line + 1, at] = jnp.sum(sums, axis=0, keepdims=True)
            stats[p][line + 1 : line + 2, at] = jnp.sum(squares, axis=0, keepdims=True)


def select_all(embeddings, slot_image, slot_view, pair_table, images):
    rows, width = embeddings.shape
    pieces = width // 128
    vmem = pl.BlockSpec(memory_space=pltpu.VMEM)
    return pl.pallas_call(
        select_kernel,
        out_shape=[jax.ShapeDtypeStruct((images, width // CHUNKS), jnp.bfloat16)] * (2 * CHUNKS)
        + [jax.ShapeDtypeStruct((images, width // 2), jnp.bfloat16)] * 4
        + [jax.ShapeDtypeStruct((8, width + 128), jnp.float32)] * 2,
        in_specs=[vmem, vmem, pl.BlockSpec(memory_space=pltpu.SMEM), pl.BlockSpec(memory_space=pl.ANY)],
        out_specs=[vmem] * (2 * CHUNKS + 6),
        scratch_shapes=[
            pltpu.VMEM((rows, width), jnp.bfloat16),
            pltpu.VMEM(((rows + 1) * pieces, 128), jnp.float32),
            pltpu.VMEM((4 * pieces * images, 128), jnp.float32),
            pltpu.VMEM((images // 8, 128), jnp.int32),
            pltpu.SMEM((images // 8, 128), jnp.int32),
            pltpu.SemaphoreType.DMA((STEPS,)),
            pltpu.SemaphoreType.DMA,
        ],
        compiler_params=pltpu.CompilerParams(vmem_limit_bytes=60 << 20),
        name="select",
    )(slot_image.reshape(1, -1), slot_view.reshape(1, -1), pair_table, embeddings)


def turn_kernel(*refs):
    for p in range(PAIRS):
        kept, kept_other, come, come_other = refs[4 * p : 4 * p + 4]
        out = refs[4 * PAIRS + p]
        images, half = kept.shape[0], kept.shape[1] // 2
        for column, sources in enumerate(((kept, kept_other), (come, come_other))):
            for line in range(2):
                for s in range(2):
                    row = (2 * line + s) * half
                    out[row : row + half, column * images : (column + 1) * images] = jnp.transpose(
                        sources[s][:, line * half : (line + 1) * half]
                    )


def turn(operands):
    images, half = operands[0].shape
    vmem = pl.BlockSpec(memory_space=pltpu.VMEM)
    return pl.pallas_call(
        turn_kernel,
        out_shape=[jax.ShapeDtypeStruct((2 * half, 2 * images), jnp.bfloat16)] * PAIRS,
        in_specs=[vmem] * (4 * PAIRS),
        out_specs=[vmem] * PAIRS,
        cost_estimate=pl.CostEstimate(flops=0, bytes_accessed=16 * half * images, transcendentals=0),
        compiler_params=pltpu.CompilerParams(vmem_limit_bytes=32 << 20),
        name="turn",
    )(*operands)


def moment_kernel(total_ref, group0, group1, rows_ref, lines_ref, work):
    width = rows_ref.shape[1]
    me = lax.axis_index("dp")
    mine = [jnp.bitwise_and(jnp.right_shift(me, bit), 1) for bit in range(2)]
    rows_ref[...] = jnp.zeros_like(rows_ref)
    lines_ref[...] = jnp.zeros_like(lines_ref)
    for p, group in enumerate((group0, group1)):
        total = total_ref[8 * p : 8 * p + 8, :]
        count = total[0:1, width : width + 1]
        amount = group[0:1, width : width + 1]
        means, roots = [], []
        for role in range(2):
            mean = total[2 * role : 2 * role + 1, :width] / count
            square = total[2 * role + 1 : 2 * role + 2, :width] / count
            means.append(mean)
            roots.append(jnp.sqrt(square - mean * mean + EPS))
        rows_ref[8 * p : 8 * p + 1, :] = means[0]
        rows_ref[8 * p + 1 : 8 * p + 2, :] = group[0:1, :width] - amount * means[0]
        rows_ref[8 * p + 2 : 8 * p + 3, :] = UNIT / (count * roots[0])
        work[0:1, :] = group[2:3, :width]
        work[1:2, :] = means[1]
        work[2:3, :] = 1.0 / roots[1]
        for m in range(4):
            over_value = mine[1 - p] if m // 2 else 1 - mine[1 - p]
            c = (m % 2) * 4 + mine[p] * (1 << p) + over_value * (2 >> p)
            lines_ref[8 * p : 8 * p + 3, m * 128 : (m + 1) * 128] = work[
                0:3, pl.ds(pl.multiple_of(c * 128, 128), 128)
            ]


def moments(total, groups, width):
    vmem = pl.BlockSpec(memory_space=pltpu.VMEM)
    return pl.pallas_call(
        moment_kernel,
        out_shape=[
            jax.ShapeDtypeStruct((8 * PAIRS, width), jnp.float32),
            jax.ShapeDtypeStruct((8 * PAIRS, width // 2), jnp.float32),
        ],
        in_specs=[vmem] * 3,
        out_specs=[vmem] * 2,
        scratch_shapes=[pltpu.VMEM((8, width), jnp.float32)],
        cost_estimate=pl.CostEstimate(flops=0, bytes_accessed=400 * width, transcendentals=0),
        name="moments",
    )(total, *groups)


def product_kernel(turned0, turned1, near0, far0, near1, far1, rows_ref, lines, lines_other, *outs):
    go, stay = outs[:PAIRS], outs[PAIRS:]
    for p, (turned, near, far) in enumerate(((turned0, near0, far0), (turned1, near1, far1))):
        depth = near.shape[0]
        half = lines.shape[1] // 2
        own, other = lines[8 * p : 8 * p + 8, :], lines_other[8 * p : 8 * p + 8, :]
        mean = rows_ref[8 * p : 8 * p + 1, :]
        shift = rows_ref[8 * p + 1 : 8 * p + 2, :]
        rate = rows_ref[8 * p + 2 : 8 * p + 3, :]
        for part in range(4):
            side, s = part // 2, part % 2
            rows = slice(part * half, (part + 1) * half)
            value = jnp.dot(turned[rows, :depth], near[...], preferred_element_type=jnp.float32)
            value += jnp.dot(turned[rows, depth:], far[...], preferred_element_type=jnp.float32)
            column = jnp.transpose((other if s else own)[:, side * half : (side + 1) * half])
            value = value - column[:, 0:1] * mean - column[:, 1:2] * shift
            value = value * (column[:, 2:3] * rate)
            if side == 0:
                value = jnp.clip(value, -60000.0, 60000.0)
            (stay if side else go)[p][s * half : (s + 1) * half, :] = value


def product(turned, near, far, rows, lines, lines_other, c):
    vmem = pl.BlockSpec(memory_space=pltpu.VMEM)
    depth, chunk = near[0].shape
    half = turned[0].shape[0] // 2
    out = jax.ShapeDtypeStruct((half, chunk), jnp.float32)
    return pl.pallas_call(
        product_kernel,
        grid=(1,),
        out_shape=[out] * (2 * PAIRS),
        in_specs=[vmem] * 6 + [pl.BlockSpec((8 * PAIRS, chunk), lambda g: (0, c))] + [vmem] * 2,
        out_specs=[vmem] * (2 * PAIRS),
        cost_estimate=pl.CostEstimate(
            flops=2 * PAIRS * 4 * half * depth * chunk, bytes_accessed=16 * half * chunk, transcendentals=0
        ),
        compiler_params=pltpu.CompilerParams(vmem_limit_bytes=32 << 20),
        name="product",
    )(*turned, near[0], far[0], near[1], far[1], rows, lines, lines_other)


def fast(embeddings, slot_image, slot_view, pair_table, images):
    width = embeddings.shape[1]
    me, core = lax.axis_index("dp"), lax.axis_index("feat")
    mine = [(me >> bit) & 1 for bit in range(4)]
    block = 128
    chosen = select_all(embeddings, slot_image, slot_view, pair_table, images)
    firsts = (chosen[:CHUNKS], chosen[CHUNKS : 2 * CHUNKS])
    kept, away, stats = (chosen[2 * CHUNKS + k : 2 * CHUNKS + k + 2] for k in (0, 2, 4))
    near_bit, over_bit = (1, 2), (2, 1)
    groups = [stats[p] + swap(stats[p], "dp", near_bit[p]) for p in range(PAIRS)]
    come = [swap(away[p], "dp", near_bit[p]) for p in range(PAIRS)]
    kept_other = [swap(kept[p], "feat", 1) for p in range(PAIRS)]
    total = jnp.concatenate(
        [groups[p] + swap(groups[p], "dp", over_bit[p]) for p in range(PAIRS)], 0
    )
    far = [[swap(firsts[p][c], "dp", near_bit[p]) for c in range(CHUNKS)] for p in range(PAIRS)]
    total = total + swap(total, "dp", 4)
    total = total + swap(total, "dp", 8)
    rows, lines = moments(total, groups, width)
    lines_other = swap(lines, "feat", 1)
    come_other = [swap(come[p], "feat", 1) for p in range(PAIRS)]
    turned = turn([v for p in range(PAIRS) for v in (kept[p], kept_other[p], come[p], come_other[p])])
    finals = []
    for c in range(CHUNKS):
        values = product(
            turned,
            [firsts[p][c] for p in range(PAIRS)],
            [far[p][c] for p in range(PAIRS)],
            rows,
            lines,
            lines_other,
            c,
        )
        chunk = width // CHUNKS
        shape = (2, 2, block, chunk)
        sent = [
            swap(values[p].astype(jnp.float16), "dp", over_bit[p]).reshape(shape)
            for p in range(PAIRS)
        ]
        stay = [values[PAIRS + p].reshape(shape) for p in range(PAIRS)]

        def pick(value, at, axis):
            return lax.dynamic_index_in_dim(value, at, axis, keepdims=False)

        def merge(own, other, at, axis):
            return pick(own, at, axis) + pick(other, at, axis).astype(jnp.float32)

        go = jnp.stack([merge(stay[p], sent[p], 1 - mine[2], 1) for p in range(PAIRS)])
        go = swap(jnp.clip(go, -60000.0, 60000.0).astype(jnp.float16), "dp", 4)
        stay = jnp.stack([merge(stay[p], sent[p], mine[2], 1) for p in range(PAIRS)])
        keep_at = mine[3] ^ core
        last = jnp.clip(merge(stay, go, 1 - keep_at, 1), -60000.0, 60000.0).astype(jnp.float16)
        last = swap(last, "dp", 8)
        finals.append(merge(stay, go, keep_at, 1) + last.astype(jnp.float32))
    return jnp.swapaxes(jnp.concatenate(finals, 2), 1, 2) * (1.0 / UNIT)


def select_plain(embeddings, slot_image, slot_view, pair_table, images):
    width = embeddings.shape[1]
    local_image = slot_image - lax.axis_index("dp") * images
    image_grid = jnp.arange(images, dtype=jnp.int32)[:, None]
    rows, stats = [], []
    for p in range(PAIRS):
        marks = [
            (local_image[None, :] == image_grid) & (slot_view[None, :] == pair_table[p, role])
            for role in range(2)
        ]
        present = jnp.any(marks[0], axis=1) & jnp.any(marks[1], axis=1)
        lines = []
        for mark in marks:
            taken = jnp.dot(
                (mark & present[:, None]).astype(jnp.bfloat16),
                embeddings,
                preferred_element_type=jnp.float32,
            )
            rows.append(taken.astype(jnp.bfloat16))
            lines += [jnp.sum(taken, axis=0), jnp.sum(taken * taken, axis=0)]
        table = jnp.pad(jnp.stack(lines), ((0, 4), (0, 128)))
        amount = jnp.sum(present.astype(jnp.float32))
        stats.append(table.at[0, width:].set(amount))
    return (*rows, *stats)


def local(embeddings, slot_image, slot_view, pair_table):
    images = embeddings.shape[0] // VIEWS
    rows, width = embeddings.shape
    dp, feat = lax.axis_size("dp"), lax.axis_size("feat")
    me, core = lax.axis_index("dp"), lax.axis_index("feat")
    if (dp, feat, width) == (16, 2, 1024) and images % 128 == 0 and rows % (32 * STEPS) == 0:
        return fast(embeddings, slot_image, slot_view, pair_table, images)
    chosen = select_plain(embeddings, slot_image, slot_view, pair_table, images)
    block = width * feat // dp
    low, high = bits_of(width // block), bits_of(feat)
    mine = [(me >> bit) & 1 for bit in range(low + high)]
    chunk = width // CHUNKS
    orders = []
    for p in range(PAIRS):
        order = list(range(low + high))
        if p % 2:
            order[:2] = order[1::-1]
        orders.append(order)
    rest_bits = list(range(2, low))[::-1]
    shape = (2,) * high + (2,) * len(rest_bits) + (block,)

    def columns(rows, bits, values):
        parts = []
        for code in range(1 << len(rest_bits)):
            start = sum(value << bit for bit, value in zip(bits, values))
            for place, bit in enumerate(rest_bits[::-1]):
                start = start + (((code >> place) & 1) << bit)
            parts.append(lax.dynamic_slice_in_dim(rows, start * block, block, 1))
        return parts

    def halves(rows, order, near_value):
        far = columns(rows, order[:2], (near_value, 1 - mine[order[1]]))
        return jnp.concatenate(far + columns(rows, order[:2], (near_value, mine[order[1]])), 1)

    def across(value):
        return jnp.stack([value] + [swap(value, "feat", s) for s in range(1, feat)], 0)

    firsts = [chosen[0], chosen[2]]
    seconds = [chosen[1], chosen[3]]
    stats = list(chosen[4:])
    kept = [halves(seconds[p], orders[p], mine[orders[p][0]]) for p in range(PAIRS)]
    away = [halves(seconds[p], orders[p], 1 - mine[orders[p][0]]) for p in range(PAIRS)]
    group = [stats[p] + swap(stats[p], "dp", 1 << orders[p][0]) for p in range(PAIRS)]
    come = [swap(away[p], "dp", 1 << orders[p][0]) for p in range(PAIRS)]
    totals = list(group)
    for step in range(1, low + high):
        totals = [totals[p] + swap(totals[p], "dp", 1 << orders[p][step]) for p in range(PAIRS)]
    pieces = [[firsts[p][:, c * chunk : (c + 1) * chunk] for c in range(CHUNKS)] for p in range(PAIRS)]
    far = [[None] * CHUNKS for _ in range(PAIRS)]
    for c in range(CHUNKS):
        for p in range(PAIRS):
            far[p][c] = swap(pieces[p][c], "dp", 1 << orders[p][0])
    kept_all = [across(kept[p]) for p in range(PAIRS)]
    come_all = [across(come[p]) for p in range(PAIRS)]
    half = kept_all[0].shape[2] // 2

    def multiply(left, right):
        return lax.dot_general(
            left, right, (((1,), (0,)), ((), ())), preferred_element_type=jnp.float32
        )

    vectors = []
    for p in range(PAIRS):
        count, amount = totals[p][0, width], group[p][0, width]
        mean = totals[p][0:4:2, :width] / count
        root = jnp.sqrt(totals[p][1:4:2, :width] / count - mean * mean + EPS)
        first_rate = UNIT / (count * root[0])
        first_shift = group[p][0, :width] - amount * mean[0]
        lines = jnp.stack([group[p][2, :width], mean[1], 1.0 / root[1]])
        lines = halves(lines, orders[p], mine[orders[p][0]])
        lines = across(lines)
        vectors.append((mean[0], first_shift, first_rate, lines))

    def product(p, c, side):
        at = slice(side * half, (side + 1) * half)
        value = multiply(kept_all[p][:, :, at], pieces[p][c]) + multiply(
            come_all[p][:, :, at], far[p][c]
        )
        mean, shift, rate, lines = vectors[p]
        span = slice(c * chunk, (c + 1) * chunk)
        lines = lines[:, :, at, None]
        value = value - lines[:, 0] * mean[span] - lines[:, 1] * shift[span]
        return (value * (lines[:, 2] * rate[span])).reshape(shape + (chunk,))

    def narrow(value):
        return jnp.clip(value, -60000.0, 60000.0).astype(jnp.float16)

    stay = [[None] * CHUNKS for _ in range(PAIRS)]
    for c in range(CHUNKS):
        for p in range(PAIRS):
            sent = swap(narrow(product(p, c, 0)), "dp", 1 << orders[p][1])
            stay[p][c] = product(p, c, 1) + sent.astype(jnp.float32)
    axes = list(range(low, low + high))[::-1] + rest_bits
    for bit in range(2, low + high):
        axis = axes.index(bit)
        axes.remove(bit)
        keep_at = mine[bit] ^ ((core >> (bit - low)) & 1) if bit >= low else mine[bit]
        for c in range(CHUNKS):
            for p in range(PAIRS):
                go = lax.dynamic_index_in_dim(stay[p][c], 1 - keep_at, axis, keepdims=False)
                sent = swap(narrow(go), "dp", 1 << bit)
                own = lax.dynamic_index_in_dim(stay[p][c], keep_at, axis, keepdims=False)
                stay[p][c] = own + sent.astype(jnp.float32)
    return jnp.stack(
        [jnp.concatenate([stay[p][c].T for c in range(CHUNKS)], 0) for p in range(PAIRS)]
    ) * (1.0 / UNIT)


def solution(mesh):
    in_specs = (P("dp", "feat"), P("dp"), P("dp"), P())
    out_specs = P(None, "feat", "dp")
    step = jax.shard_map(local, mesh=mesh, in_specs=in_specs, out_specs=out_specs, check_vma=False)
    if dict(mesh.shape) != {"dp": 16, "feat": 2}:
        return step
    return step
```

```python
import jax
import jax.numpy as jnp
from jax import lax
from jax.experimental import pallas as pl
from jax.experimental.pallas import tpu as pltpu
from jax.sharding import PartitionSpec as P

VIEWS = 10
PAIRS = 2
EPS = 1e-05
CHUNKS = 4
PARTS = 2
STEPS = 10
UNIT = 16384.0


def swap(value, axis, mask):
    size = lax.axis_size(axis)
    return lax.ppermute(value, axis, [(k, k ^ mask) for k in range(size)])


def bits_of(size):
    return size.bit_length() - 1


def select_kernel(image_ref, view_ref, pair_ref, emb_ref, *refs):
    firsts = (refs[:CHUNKS], refs[CHUNKS : 2 * CHUNKS])
    kept, away, stats = (refs[2 * CHUNKS + k : 2 * CHUNKS + k + 2] for k in (0, 2, 4))
    raw, wide, held, turned, slots, sem, slot_sem = refs[2 * CHUNKS + 6 :]
    rows, width = raw.shape
    pieces = width // 128
    images = firsts[0][0].shape[0]
    step = rows // STEPS

    def fetch(k):
        part = pl.ds(k * step, step)
        return pltpu.make_async_copy(emb_ref.at[part, :], raw.at[part, :], sem.at[k])

    for k in range(STEPS):
        fetch(k).start()
    image = image_ref[...] - lax.axis_index("dp") * images
    view = view_ref[...]
    groups = images // 16
    upper = lax.broadcasted_iota(jnp.int32, (groups, rows), 0)
    hits = jnp.where(upper == jnp.right_shift(image, 4), 1.0, 0.0).astype(jnp.bfloat16)
    lower = jnp.bitwise_and(image, 15) * 16 + view
    line = lax.broadcasted_iota(jnp.int32, (96, 1), 0)
    place = lax.broadcasted_iota(jnp.int32, (32, rows), 1)
    values = jnp.concatenate(
        [jnp.right_shift(place, 6), jnp.bitwise_and(place, 63), jnp.ones_like(place)], 0
    ).astype(jnp.float32)
    found = []
    for role in range(2):
        wanted = jnp.bitwise_and(line, 15) * 16 + jnp.where(
            jnp.bitwise_and(line, 16) == 0, pair_ref[0, role], pair_ref[1, role]
        )
        marks = jnp.where(wanted == lower, values, 0.0).astype(jnp.bfloat16)
        marks = jnp.concatenate([marks, jnp.zeros((32, rows), jnp.bfloat16)], 0)
        found.append(
            lax.dot_general(
                hits, marks, (((1,), (1,)), ((), ())), preferred_element_type=jnp.float32
            )
        )
    both = pltpu.roll(found[0], 64, 1) * pltpu.roll(found[1], 64, 1) > 0.5
    for ref in stats:
        ref[...] = jnp.zeros_like(ref)
    lanes = lax.broadcasted_iota(jnp.int32, (groups, 128), 1)
    for p in range(2):
        mine = both & (lanes >= 16 * p) & (lanes < 16 * p + 16)
        amount = jnp.sum(jnp.sum(mine.astype(jnp.float32), axis=0, keepdims=True), axis=1, keepdims=True)
        stats[p][0:1, width : width + 128] = jnp.broadcast_to(amount, (1, 128))
    for role in range(2):
        slot = jnp.minimum(found[role] * 64.0 + pltpu.roll(found[role], 96, 1), float(rows))
        turned[role * groups : (role + 1) * groups, :] = jnp.where(both, slot, float(rows)).astype(
            jnp.int32
        )
    to_scalar = pltpu.make_async_copy(turned, slots, slot_sem)
    to_scalar.start()
    wide[pl.ds(rows * pieces, pieces), :] = jnp.zeros((pieces, 128), jnp.float32)
    for k in range(STEPS):
        fetch(k).wait()

        def widen(t, carry):
            start = pl.multiple_of(k * step + t * 32, 32)
            for c in range(pieces):
                wide[pl.ds(start * pieces + c, 32, stride=pieces), :] = raw[
                    pl.ds(start, 32), c * 128 : (c + 1) * 128
                ].astype(jnp.float32)
            return carry

        lax.fori_loop(0, step // 32, widen, 0)
    to_scalar.wait()

    def gather(t, carry):
        for u in range(16):
            n = t * 16 + u
            for k in range(4):
                slot = slots[(k % 2) * groups + t, (k // 2) * 16 + u]
                held[pl.ds(pl.multiple_of((k * images + n) * pieces, pieces), pieces), :] = wide[
                    pl.ds(pl.multiple_of(slot * pieces, pieces), pieces), :
                ]
        return carry

    lax.fori_loop(0, groups, gather, 0)
    me = lax.axis_index("dp")
    mine = [jnp.bitwise_and(jnp.right_shift(me, bit), 1) for bit in range(4)]
    span = width // CHUNKS // 128
    for k in range(4):
        p, line = k // 2, 2 * (k % 2)
        for m in range(pieces):
            if k % 2:
                near, over, rest = m // 4, (m // 2) % 2, m % 2
                near_value = mine[p] if near else 1 - mine[p]
                over_value = mine[1 - p] if over else 1 - mine[1 - p]
                rest_value = mine[2] if rest else 1 - mine[2]
                c = rest_value * 4 + near_value * (1 << p) + over_value * (2 >> p)
                out = (kept if near else away)[p]
                lane = (m % 4) * 128
            else:
                c, out, lane = m, firsts[p][m // span], (m % span) * 128

            def emit(t, carry):
                sums, squares = carry
                start = pl.multiple_of(t * 128, 128)
                value = held[pl.ds((k * images + start) * pieces + c, 128, stride=pieces), :]
                out[pl.ds(start, 128), lane : lane + 128] = value.astype(jnp.bfloat16)
                value = value.reshape(16, 8, 128)
                return sums + value.sum(0), squares + (value * value).sum(0)

            zero = jnp.zeros((8, 128), jnp.float32)
            sums, squares = lax.fori_loop(0, images // 128, emit, (zero, zero))
            at = pl.ds(pl.multiple_of(c * 128, 128), 128)
            stats[p][line : line + 1, at] = jnp.sum(sums, axis=0, keepdims=True)
            stats[p][line + 1 : line + 2, at] = jnp.sum(squares, axis=0, keepdims=True)


def select_all(embeddings, slot_image, slot_view, pair_table, images):
    rows, width = embeddings.shape
    pieces = width // 128
    vmem = pl.BlockSpec(memory_space=pltpu.VMEM)
    return pl.pallas_call(
        select_kernel,
        out_shape=[jax.ShapeDtypeStruct((images, width // CHUNKS), jnp.bfloat16)] * (2 * CHUNKS)
        + [jax.ShapeDtypeStruct((images, width // 2), jnp.bfloat16)] * 4
        + [jax.ShapeDtypeStruct((8, width + 128), jnp.float32)] * 2,
        in_specs=[vmem, vmem, pl.BlockSpec(memory_space=pltpu.SMEM), pl.BlockSpec(memory_space=pl.ANY)],
        out_specs=[vmem] * (2 * CHUNKS + 6),
        scratch_shapes=[
            pltpu.VMEM((rows, width), jnp.bfloat16),
            pltpu.VMEM(((rows + 1) * pieces, 128), jnp.float32),
            pltpu.VMEM((4 * pieces * images, 128), jnp.float32),
            pltpu.VMEM((images // 8, 128), jnp.int32),
            pltpu.SMEM((images // 8, 128), jnp.int32),
            pltpu.SemaphoreType.DMA((STEPS,)),
            pltpu.SemaphoreType.DMA,
        ],
        compiler_params=pltpu.CompilerParams(vmem_limit_bytes=60 << 20),
        name="select",
    )(slot_image.reshape(1, -1), slot_view.reshape(1, -1), pair_table, embeddings)


def kept_core():
    return jnp.bitwise_and(jnp.right_shift(lax.axis_index("dp"), 3), 1) == lax.axis_index("feat")


def turn_kernel(*refs):
    own_at = jnp.where(kept_core(), 1, 0)
    for p in range(PAIRS):
        kept, kept_other, come, come_other = refs[4 * p : 4 * p + 4]
        out = refs[4 * PAIRS + p]
        images, block = kept.shape[0], kept.shape[1] // 4
        for column, sources in enumerate(((kept, kept_other), (come, come_other))):
            for m in range(4):
                for s in range(2):
                    at = (2 * m + (1 - own_at if s else own_at)) * block
                    out[
                        pl.ds(pl.multiple_of(at, block), block),
                        column * images : (column + 1) * images,
                    ] = jnp.transpose(sources[s][:, m * block : (m + 1) * block])


def turn(operands):
    images, half = operands[0].shape
    vmem = pl.BlockSpec(memory_space=pltpu.VMEM)
    return pl.pallas_call(
        turn_kernel,
        out_shape=[jax.ShapeDtypeStruct((2 * half, 2 * images), jnp.bfloat16)] * PAIRS,
        in_specs=[vmem] * (4 * PAIRS),
        out_specs=[vmem] * PAIRS,
        cost_estimate=pl.CostEstimate(flops=0, bytes_accessed=16 * half * images, transcendentals=0),
        compiler_params=pltpu.CompilerParams(vmem_limit_bytes=32 << 20),
        name="turn",
    )(*operands)


def moment_kernel(total_ref, group0, group1, rows_ref, lines_ref, work):
    width = rows_ref.shape[1]
    me = lax.axis_index("dp")
    mine = [jnp.bitwise_and(jnp.right_shift(me, bit), 1) for bit in range(4)]
    rows_ref[...] = jnp.zeros_like(rows_ref)
    lines_ref[...] = jnp.zeros_like(lines_ref)
    for p, group in enumerate((group0, group1)):
        total = total_ref[8 * p : 8 * p + 8, :]
        count = total[0:1, width : width + 1]
        amount = group[0:1, width : width + 1]
        means, roots = [], []
        for role in range(2):
            mean = total[2 * role : 2 * role + 1, :width] / count
            square = total[2 * role + 1 : 2 * role + 2, :width] / count
            means.append(mean)
            roots.append(jnp.sqrt(square - mean * mean + EPS))
        rows_ref[8 * p : 8 * p + 1, :] = means[0]
        rows_ref[8 * p + 1 : 8 * p + 2, :] = group[0:1, :width] - amount * means[0]
        rows_ref[8 * p + 2 : 8 * p + 3, :] = UNIT / (count * roots[0])
        work[0:1, :] = group[2:3, :width]
        work[1:2, :] = means[1]
        work[2:3, :] = 1.0 / roots[1]
        for m in range(4):
            over_value = mine[1 - p] if m // 2 else 1 - mine[1 - p]
            rest_value = mine[2] if m % 2 else 1 - mine[2]
            c = rest_value * 4 + mine[p] * (1 << p) + over_value * (2 >> p)
            lines_ref[8 * p : 8 * p + 3, m * 128 : (m + 1) * 128] = work[
                0:3, pl.ds(pl.multiple_of(c * 128, 128), 128)
            ]


def moments(total, groups, width):
    vmem = pl.BlockSpec(memory_space=pltpu.VMEM)
    return pl.pallas_call(
        moment_kernel,
        out_shape=[
            jax.ShapeDtypeStruct((8 * PAIRS, width), jnp.float32),
            jax.ShapeDtypeStruct((8 * PAIRS, width // 2), jnp.float32),
        ],
        in_specs=[vmem] * 3,
        out_specs=[vmem] * 2,
        scratch_shapes=[pltpu.VMEM((8, width), jnp.float32)],
        cost_estimate=pl.CostEstimate(flops=0, bytes_accessed=400 * width, transcendentals=0),
        name="moments",
    )(total, *groups)


def product_kernel(turned0, turned1, near0, far0, near1, far1, rows_ref, lines, lines_other, *outs):
    go, stay = outs[:PAIRS], outs[PAIRS:]
    own_kept = kept_core()
    for p, (turned, near, far) in enumerate(((turned0, near0, far0), (turned1, near1, far1))):
        block = lines.shape[1] // 4
        own, other = lines[8 * p : 8 * p + 8, :], lines_other[8 * p : 8 * p + 8, :]
        sources = (jnp.where(own_kept, other, own), jnp.where(own_kept, own, other))
        mean = rows_ref[8 * p : 8 * p + 1, :]
        shift = rows_ref[8 * p + 1 : 8 * p + 2, :]
        rate = rows_ref[8 * p + 2 : 8 * p + 3, :]
        right = jnp.concatenate([near[...], far[...]], 0)
        for part in range(8):
            m, z = part // 2, part % 2
            value = jnp.dot(
                turned[part * block : (part + 1) * block, :], right, preferred_element_type=jnp.float32
            )
            column = jnp.transpose(sources[z][:, m * block : (m + 1) * block])
            value = value - column[:, 0:1] * mean - column[:, 1:2] * shift
            value = value * (column[:, 2:3] * rate)
            if part < 4:
                value = jnp.clip(value, -60000.0, 60000.0)
                go[p][part * block : (part + 1) * block, :] = value
            else:
                stay[p][(part - 4) * block : (part - 3) * block, :] = value


def product(turned, near, far, rows, lines, lines_other, c):
    vmem = pl.BlockSpec(memory_space=pltpu.VMEM)
    depth, chunk = near[0].shape
    half = turned[0].shape[0] // 2
    out = jax.ShapeDtypeStruct((half, chunk), jnp.float32)
    return pl.pallas_call(
        product_kernel,
        grid=(1,),
        out_shape=[out] * (2 * PAIRS),
        in_specs=[vmem] * 6 + [pl.BlockSpec((8 * PAIRS, chunk), lambda g: (0, c))] + [vmem] * 2,
        out_specs=[vmem] * (2 * PAIRS),
        cost_estimate=pl.CostEstimate(
            flops=2 * PAIRS * 4 * half * depth * chunk, bytes_accessed=16 * half * chunk, transcendentals=0
        ),
        compiler_params=pltpu.CompilerParams(vmem_limit_bytes=32 << 20),
        name="product",
    )(*turned, near[0], far[0], near[1], far[1], rows, lines, lines_other)


def finish_kernel(*refs):
    out = refs[-1]
    chunk = refs[0].shape[2]
    for c, ref in enumerate(refs[:-1]):
        for p in range(PAIRS):
            out[p, c * chunk : (c + 1) * chunk, :] = jnp.transpose(ref[p]) * (1.0 / UNIT)


def finish(parts):
    pairs, block, chunk = parts[0].shape
    vmem = pl.BlockSpec(memory_space=pltpu.VMEM)
    return pl.pallas_call(
        finish_kernel,
        out_shape=jax.ShapeDtypeStruct((pairs, chunk * len(parts), block), jnp.float32),
        in_specs=[vmem] * len(parts),
        out_specs=vmem,
        name="finish",
    )(*parts)


def fast(embeddings, slot_image, slot_view, pair_table, images):
    width = embeddings.shape[1]
    block = 128
    chosen = select_all(embeddings, slot_image, slot_view, pair_table, images)
    firsts = (chosen[:CHUNKS], chosen[CHUNKS : 2 * CHUNKS])
    kept, away, stats = (chosen[2 * CHUNKS + k : 2 * CHUNKS + k + 2] for k in (0, 2, 4))
    near_bit, over_bit = (1, 2), (2, 1)
    groups = [stats[p] + swap(stats[p], "dp", near_bit[p]) for p in range(PAIRS)]
    come = [swap(away[p], "dp", near_bit[p]) for p in range(PAIRS)]
    kept_other = [swap(kept[p], "feat", 1) for p in range(PAIRS)]
    total = jnp.concatenate(
        [groups[p] + swap(groups[p], "dp", over_bit[p]) for p in range(PAIRS)], 0
    )
    far = [[swap(firsts[p][c], "dp", near_bit[p]) for c in range(CHUNKS)] for p in range(PAIRS)]
    total = total + swap(total, "dp", 4)
    total = total + swap(total, "dp", 8)
    rows, lines = moments(total, groups, width)
    lines_other = swap(lines, "feat", 1)
    come_other = [swap(come[p], "feat", 1) for p in range(PAIRS)]
    turned = turn([v for p in range(PAIRS) for v in (kept[p], kept_other[p], come[p], come_other[p])])
    finals = []
    for c in range(CHUNKS):
        values = product(
            turned,
            [firsts[p][c] for p in range(PAIRS)],
            [far[p][c] for p in range(PAIRS)],
            rows,
            lines,
            lines_other,
            c,
        )
        sent = [swap(values[p].astype(jnp.float16), "dp", over_bit[p]) for p in range(PAIRS)]
        both = range(PAIRS)

        def narrow(value):
            return jnp.clip(value, -60000.0, 60000.0).astype(jnp.float16)

        def merge(p, at):
            return values[PAIRS + p][at] + sent[p][at].astype(jnp.float32)

        head, rest = slice(0, 2 * block), slice(2 * block, 4 * block)
        go = swap(jnp.stack([narrow(merge(p, head)) for p in both]), "dp", 4)
        stay = jnp.stack([merge(p, rest) for p in both])
        last = narrow(stay[:, :block] + go[:, :block].astype(jnp.float32))
        last = swap(last, "dp", 8)
        finals.append(
            stay[:, block:] + go[:, block:].astype(jnp.float32) + last.astype(jnp.float32)
        )
    return finish(finals)


def select_plain(embeddings, slot_image, slot_view, pair_table, images):
    width = embeddings.shape[1]
    local_image = slot_image - lax.axis_index("dp") * images
    image_grid = jnp.arange(images, dtype=jnp.int32)[:, None]
    rows, stats = [], []
    for p in range(PAIRS):
        marks = [
            (local_image[None, :] == image_grid) & (slot_view[None, :] == pair_table[p, role])
            for role in range(2)
        ]
        present = jnp.any(marks[0], axis=1) & jnp.any(marks[1], axis=1)
        lines = []
        for mark in marks:
            taken = jnp.dot(
                (mark & present[:, None]).astype(jnp.bfloat16),
                embeddings,
                preferred_element_type=jnp.float32,
            )
            rows.append(taken.astype(jnp.bfloat16))
            lines += [jnp.sum(taken, axis=0), jnp.sum(taken * taken, axis=0)]
        table = jnp.pad(jnp.stack(lines), ((0, 4), (0, 128)))
        amount = jnp.sum(present.astype(jnp.float32))
        stats.append(table.at[0, width:].set(amount))
    return (*rows, *stats)


def local(embeddings, slot_image, slot_view, pair_table):
    images = embeddings.shape[0] // VIEWS
    rows, width = embeddings.shape
    dp, feat = lax.axis_size("dp"), lax.axis_size("feat")
    me, core = lax.axis_index("dp"), lax.axis_index("feat")
    if (dp, feat, width) == (16, 2, 1024) and images % 128 == 0 and rows % (32 * STEPS) == 0:
        return fast(embeddings, slot_image, slot_view, pair_table, images)
    chosen = select_plain(embeddings, slot_image, slot_view, pair_table, images)
    block = width * feat // dp
    low, high = bits_of(width // block), bits_of(feat)
    mine = [(me >> bit) & 1 for bit in range(low + high)]
    chunk = width // PARTS
    orders = []
    for p in range(PAIRS):
        order = list(range(low + high))
        if p % 2:
            order[:2] = order[1::-1]
        orders.append(order)
    rest_bits = list(range(2, low))[::-1]
    shape = (2,) * high + (2,) * len(rest_bits) + (block,)

    def columns(rows, bits, values):
        parts = []
        for code in range(1 << len(rest_bits)):
            start = sum(value << bit for bit, value in zip(bits, values))
            for place, bit in enumerate(rest_bits[::-1]):
                start = start + (((code >> place) & 1) << bit)
            parts.append(lax.dynamic_slice_in_dim(rows, start * block, block, 1))
        return parts

    def halves(rows, order, near_value):
        far = columns(rows, order[:2], (near_value, 1 - mine[order[1]]))
        return jnp.concatenate(far + columns(rows, order[:2], (near_value, mine[order[1]])), 1)

    def across(value):
        return jnp.stack([value] + [swap(value, "feat", s) for s in range(1, feat)], 0)

    firsts = [chosen[0], chosen[2]]
    seconds = [chosen[1], chosen[3]]
    stats = list(chosen[4:])
    kept = [halves(seconds[p], orders[p], mine[orders[p][0]]) for p in range(PAIRS)]
    away = [halves(seconds[p], orders[p], 1 - mine[orders[p][0]]) for p in range(PAIRS)]
    group = [stats[p] + swap(stats[p], "dp", 1 << orders[p][0]) for p in range(PAIRS)]
    come = [swap(away[p], "dp", 1 << orders[p][0]) for p in range(PAIRS)]
    totals = list(group)
    for step in range(1, low + high):
        totals = [totals[p] + swap(totals[p], "dp", 1 << orders[p][step]) for p in range(PAIRS)]
    pieces = [[firsts[p][:, c * chunk : (c + 1) * chunk] for c in range(PARTS)] for p in range(PAIRS)]
    far = [[None] * PARTS for _ in range(PAIRS)]
    for c in range(PARTS):
        for p in range(PAIRS):
            far[p][c] = swap(pieces[p][c], "dp", 1 << orders[p][0])
    kept_all = [across(kept[p]) for p in range(PAIRS)]
    come_all = [across(come[p]) for p in range(PAIRS)]
    half = kept_all[0].shape[2] // 2

    def multiply(left, right):
        return lax.dot_general(
            left, right, (((1,), (0,)), ((), ())), preferred_element_type=jnp.float32
        )

    vectors = []
    for p in range(PAIRS):
        count, amount = totals[p][0, width], group[p][0, width]
        mean = totals[p][0:4:2, :width] / count
        root = jnp.sqrt(totals[p][1:4:2, :width] / count - mean * mean + EPS)
        first_rate = UNIT / (count * root[0])
        first_shift = group[p][0, :width] - amount * mean[0]
        lines = jnp.stack([group[p][2, :width], mean[1], 1.0 / root[1]])
        lines = halves(lines, orders[p], mine[orders[p][0]])
        lines = across(lines)
        vectors.append((mean[0], first_shift, first_rate, lines))

    def product(p, c, side):
        at = slice(side * half, (side + 1) * half)
        value = multiply(kept_all[p][:, :, at], pieces[p][c]) + multiply(
            come_all[p][:, :, at], far[p][c]
        )
        mean, shift, rate, lines = vectors[p]
        span = slice(c * chunk, (c + 1) * chunk)
        lines = lines[:, :, at, None]
        value = value - lines[:, 0] * mean[span] - lines[:, 1] * shift[span]
        return (value * (lines[:, 2] * rate[span])).reshape(shape + (chunk,))

    def narrow(value):
        return jnp.clip(value, -60000.0, 60000.0).astype(jnp.float16)

    stay = [[None] * PARTS for _ in range(PAIRS)]
    for c in range(PARTS):
        for p in range(PAIRS):
            sent = swap(narrow(product(p, c, 0)), "dp", 1 << orders[p][1])
            stay[p][c] = product(p, c, 1) + sent.astype(jnp.float32)
    axes = list(range(low, low + high))[::-1] + rest_bits
    for bit in range(2, low + high):
        axis = axes.index(bit)
        axes.remove(bit)
        keep_at = mine[bit] ^ ((core >> (bit - low)) & 1) if bit >= low else mine[bit]
        for c in range(PARTS):
            for p in range(PAIRS):
                go = lax.dynamic_index_in_dim(stay[p][c], 1 - keep_at, axis, keepdims=False)
                sent = swap(narrow(go), "dp", 1 << bit)
                own = lax.dynamic_index_in_dim(stay[p][c], keep_at, axis, keepdims=False)
                stay[p][c] = own + sent.astype(jnp.float32)
    return jnp.stack(
        [jnp.concatenate([stay[p][c].T for c in range(PARTS)], 0) for p in range(PAIRS)]
    ) * (1.0 / UNIT)


def solution(mesh):
    in_specs = (P("dp", "feat"), P("dp"), P("dp"), P())
    out_specs = P(None, "feat", "dp")
    step = jax.shard_map(local, mesh=mesh, in_specs=in_specs, out_specs=out_specs, check_vma=False)
    if dict(mesh.shape) != {"dp": 16, "feat": 2}:
        return step

    return step
```
